32 devices in a mesh: ctx: 8 (over y, x, core), tp: 4 (over z).
Axes of the slice: x: 2, y: 2, z: 4, core: 2. Of those that a mesh axis runs over, the one named last changes fastest.
Arguments:
- tokens: bfloat16 [4096, 4096], P('ctx', 'tp'), may hold values from -6 to 6
- norm_gain: float32 [4096], replicated, may hold values from 0.5 to 1.5
- proj_weight: bfloat16 [3, 4096, 2048], P(None, None, 'tp'), may hold values from -0.09375 to 0.09375
- short_taps: float32 [3, 3, 2048], P(None, None, 'tp'), may hold values from -1 to 1
- long_filter: float32 [4096, 2048], P('ctx', 'tp'), may hold values from -0.09375 to 0.09375
- skip_gain: float32 [2048], P('tp'), may hold values from -1 to 1
Outputs:
- output: bfloat16 [4096, 2048], P('ctx', 'tp')
The draws below stay inside these ranges and needn't reach their ends.
All inputs are finite; a program needn't handle non-finite values.
Results may differ from the reference program's by a relative error of at most 0.0081.
Values may be sent and summed in bfloat16 or wider, within the bound.
A program may use at most 128 MiB of HBM per device.

```python
import jax
import jax.numpy as jnp
from jax import lax

D = 4096
CH = 2048
SEQ = 4096
N_TP = 4


def level_of(stream_key, dims, cuts, smallest, largest):
    factor_of = 1.0
    for position, blocks in cuts:
        heights = jax.random.uniform(jax.random.fold_in(jax.random.fold_in(stream_key, 6), position), (blocks,), jnp.float32, smallest / len(cuts), largest / len(cuts))
        factor_of = factor_of * jnp.repeat(jnp.exp(heights), dims[position] // blocks).reshape((-1,) + (1,) * (len(dims) - 1 - position))
    return factor_of


def noise(rng, dims, scale, bound, cuts=(), held_as=jnp.bfloat16):
    entries = jax.random.normal(rng, dims, jnp.float32) * scale
    if len(cuts) > 0:
        entries = level_of(rng, dims, cuts, -0.22, 0.18) * entries
    return jnp.clip(entries, min=-bound, max=bound).astype(held_as)


def setup_inputs(seed: int = 0) -> dict:
    arg_keys = jax.random.split(jax.random.key(seed), 7)
    tokens = noise(arg_keys[0], (SEQ, D), 1.0, 6.0, ((0, 8), (1, 4)))
    norm_gain = jnp.clip(1.0 + 0.1 * jax.random.normal(arg_keys[1], (D,), jnp.float32), 0.5, 1.5)
    proj_weight = noise(arg_keys[2], (3, D, CH), D ** -0.5, 0.09375, ((2, 4),))
    short_taps = jnp.clip(jax.random.uniform(arg_keys[3], (3, 3, CH), jnp.float32, -1.0, 1.0) * level_of(arg_keys[3], (3, 3, CH), ((2, 4),), -0.4, 0.0), -1.0, 1.0)
    long_filter = noise(arg_keys[4], (SEQ, CH), SEQ ** -0.5, 0.09375, ((0, 8), (1, 4)), jnp.float32)
    skip_gain = jnp.clip(jax.random.uniform(arg_keys[5], (CH,), jnp.float32, -1.0, 1.0) * level_of(arg_keys[5], (CH,), ((0, 4),), -0.4, 0.0), -1.0, 1.0)
    return dict(tokens=tokens, norm_gain=norm_gain, proj_weight=proj_weight, short_taps=short_taps, long_filter=long_filter, skip_gain=skip_gain)


def reference(tokens, norm_gain, proj_weight, short_taps, long_filter, skip_gain):
    widened = tokens.astype(jnp.float32)
    scaling = lax.rsqrt(lax.optimization_barrier(jnp.mean(widened * widened, axis=1, keepdims=True)) + 1e-06)
    normed = (widened * scaling * norm_gain).astype(jnp.bfloat16)
    projected = jnp.stack([jnp.dot(normed, proj_weight[which], preferred_element_type=jnp.float32) for which in range(3)]).astype(jnp.bfloat16)
    padded = jnp.pad(projected.astype(jnp.float32), ((0, 0), (2, 0), (0, 0)))
    branch = short_taps[:, 0, None, :] * padded[:, 2:, :] + short_taps[:, 1, None, :] * padded[:, 1:-1, :] + short_taps[:, 2, None, :] * padded[:, :-2, :]
    mixed_field = branch[1] * branch[2]
    seq_length = tokens.shape[0]
    group_width = CH // N_TP
    group_count = CH // group_width

    def convolve(group_number):
        first = (group_number * group_width).astype(jnp.int32)
        signal = lax.dynamic_slice_in_dim(mixed_field, first, group_width, 1)
        impulse = lax.dynamic_slice_in_dim(long_filter, first, group_width, 1)
        spectrum = jnp.fft.rfft(signal, n=2 * seq_length, axis=0) * jnp.fft.rfft(impulse, n=2 * seq_length, axis=0)
        return jnp.fft.irfft(spectrum, n=2 * seq_length, axis=0)[:seq_length].astype(jnp.float32)
    pieces = lax.map(convolve, jnp.arange(group_count, dtype=jnp.int32))
    convolved = jnp.transpose(pieces, (1, 0, 2)).reshape(seq_length, CH)
    return (branch[0] * (convolved + skip_gain * mixed_field)).astype(jnp.bfloat16)
```

```python
import functools
import math

import jax
import jax.numpy as jnp
import numpy as np
from jax import lax
from jax.experimental import pallas as pl
from jax.experimental.pallas import tpu as pltpu
from jax.sharding import PartitionSpec as P

highest = lax.Precision.HIGHEST


def from_behind(array, axis, by):
    devices = lax.axis_size(axis)
    pairs = [(i, i + by) for i in range(devices) if 0 <= i + by < devices]
    return lax.ppermute(array, axis, pairs)


def twist_tables(part_count, row_count):
    row = lax.optimization_barrier(jnp.arange(row_count, dtype=jnp.int32))
    turn = jnp.arange(part_count + 1, dtype=jnp.int32)[:, None] * row[None, :]
    angles = turn.astype(jnp.float32) * (math.pi / (part_count * row_count))
    return (jnp.cos(angles), jnp.sin(angles))


def inner_tables(row_count):
    row = lax.optimization_barrier(jnp.arange(row_count, dtype=jnp.int32))
    turn = row[:, None] * row[None, :] % row_count
    angles = turn.astype(jnp.float32) * (2.0 * math.pi / row_count)
    cos, sin = jnp.cos(angles), jnp.sin(angles)
    forward = jnp.block([[cos, -sin], [sin, cos]])
    backward = jnp.block([[cos, sin], [-sin, cos]])
    return lax.optimization_barrier((forward, forward.astype(jnp.bfloat16), backward.astype(jnp.bfloat16)))


def turn_of(a, k, part_count):
    step = a * k % (2 * part_count)
    cos = math.cos(math.pi * step / part_count)
    sin = math.sin(math.pi * step / part_count)
    return (0.0 if abs(cos) < 1e-12 else cos, 0.0 if abs(sin) < 1e-12 else sin)


def weighted(terms):
    total = None
    for factor, term in terms:
        if factor == 0.0:
            continue
        scaled = term if factor == 1.0 else -term if factor == -1.0 else factor * term
        total = scaled if total is None else total + scaled
    return total


def filter_spectrum(taps, part_count, twist, forward):
    channels, row_count = taps.shape[1:]
    twist_cos, twist_sin = twist
    turn = np.arange(part_count + 1)[:, None] * np.arange(part_count)[None, :] % (2 * part_count)
    outer_cos = np.cos(turn * (math.pi / part_count)).astype(np.float32)
    outer_sin = np.sin(turn * (math.pi / part_count)).astype(np.float32)
    real = jnp.einsum("ka,acm->kcm", outer_cos, taps, precision=highest)
    imag = -jnp.einsum("ka,acm->kcm", outer_sin, taps, precision=highest)
    cos, sin = twist_cos[:, None, :], twist_sin[:, None, :]
    turned = jnp.concatenate([real * cos + imag * sin, imag * cos - real * sin], axis=2)
    spectrum = jnp.einsum("kcm,mn->kcn", turned, forward, precision=highest)
    share = np.full((part_count + 1, 1, 1), 2.0, np.float32)
    share[0] = share[part_count] = 1.0
    return spectrum * (share / (2 * part_count * row_count))


def convolve_kernel(part_count, x_ref, gain_ref, cos_ref, sin_ref, forward_ref, backward_ref, y_ref, turned_ref, back_ref):
    channels, row_count = x_ref.shape[1:]
    low, high = pl.ds(0, row_count), pl.ds(row_count, row_count)
    parts = [x_ref[a].astype(jnp.float32) for a in range(part_count)]
    for k in range(part_count + 1):
        turns = [turn_of(a, k, part_count) for a in range(part_count)]
        cos, sin = cos_ref[pl.ds(k, 1), :], sin_ref[pl.ds(k, 1), :]
        real = weighted([(t[0], p) for t, p in zip(turns, parts)])
        imag = weighted([(-t[1], p) for t, p in zip(turns, parts)])
        rows = pl.ds(k * channels, channels)
        if imag is None:
            turned_ref[rows, low] = (real * cos).astype(jnp.bfloat16)
            turned_ref[rows, high] = (-real * sin).astype(jnp.bfloat16)
        else:
            turned_ref[rows, low] = (real * cos + imag * sin).astype(jnp.bfloat16)
            turned_ref[rows, high] = (imag * cos - real * sin).astype(jnp.bfloat16)
    spec = jnp.dot(turned_ref[...], forward_ref[...], preferred_element_type=jnp.float32)
    gain = gain_ref[...]
    spec_real, spec_imag = spec[:, :row_count], spec[:, row_count:]
    gain_real, gain_imag = gain[:, :row_count], gain[:, row_count:]
    turned_ref[:, low] = (spec_real * gain_real - spec_imag * gain_imag).astype(jnp.bfloat16)
    turned_ref[:, high] = (spec_real * gain_imag + spec_imag * gain_real).astype(jnp.bfloat16)
    back_ref[...] = jnp.dot(turned_ref[...], backward_ref[...], preferred_element_type=jnp.float32)
    for k in range(part_count + 1):
        cos, sin = cos_ref[pl.ds(k, 1), :], sin_ref[pl.ds(k, 1), :]
        rows = pl.ds(k * channels, channels)
        real, imag = back_ref[rows, low], back_ref[rows, high]
        back_ref[rows, low] = real * cos - imag * sin
        if 0 < k < part_count:
            back_ref[rows, high] = real * sin + imag * cos
    for a in range(part_count):
        terms = []
        for k in range(part_count + 1):
            cos, sin = turn_of(a, k, part_count)
            rows = pl.ds(k * channels, channels)
            terms.append((cos, back_ref[rows, low]))
            if sin != 0.0:
                terms.append((-sin, back_ref[rows, high]))
        y_ref[a] = weighted(terms).astype(jnp.bfloat16)


def convolve(signal, spectrum, twist, forward, backward):
    part_count, channels, row_count = signal.shape
    rows = (part_count + 1) * channels
    return pl.pallas_call(
        functools.partial(convolve_kernel, part_count),
        out_shape=jax.ShapeDtypeStruct(signal.shape, jnp.bfloat16),
        in_specs=[pl.BlockSpec(memory_space=pltpu.VMEM)] * 6,
        out_specs=pl.BlockSpec(memory_space=pltpu.VMEM),
        scratch_shapes=[
            pltpu.VMEM((rows, 2 * row_count), jnp.bfloat16),
            pltpu.VMEM((rows, 2 * row_count), jnp.float32),
        ],
        compiler_params=pltpu.CompilerParams(vmem_limit_bytes=40 << 20),
        name="convolve",
    )(
        signal,
        spectrum.reshape(rows, 2 * row_count),
        *twist,
        forward,
        backward,
    )


def body(tokens, norm_gain, proj_weight, short_taps, long_filter, skip_gain):
    part_count = lax.axis_size("ctx")
    row_count, channels = long_filter.shape
    spread = (part_count, channels // part_count, row_count)
    gathered = lax.all_gather(tokens, "tp", axis=1, tiled=True)
    taps = lax.all_to_all(long_filter.T.reshape(spread), "ctx", split_axis=0, concat_axis=0, tiled=True)
    twist = twist_tables(part_count, row_count)
    inner, forward, backward = inner_tables(row_count)
    spectrum = filter_spectrum(taps, part_count, twist, inner)
    gathered, spectrum = lax.optimization_barrier((gathered, spectrum))
    widened = gathered.astype(jnp.float32)
    scaling = lax.rsqrt(jnp.mean(widened * widened, axis=1, keepdims=True) + 1e-06)
    normed = (widened * scaling * norm_gain).astype(jnp.bfloat16)
    projected = jnp.einsum(
        "td,bdc->bct", normed, proj_weight, preferred_element_type=jnp.float32
    ).astype(jnp.bfloat16)
    previous = from_behind(projected[:, :, -2:], "ctx", 1)
    extended = jnp.concatenate([previous, projected], axis=2).astype(jnp.float32)
    branch = (
        short_taps[:, 0, :, None] * extended[:, :, 2:]
        + short_taps[:, 1, :, None] * extended[:, :, 1:-1]
        + short_taps[:, 2, :, None] * extended[:, :, :-2]
    )
    mixed = branch[1] * branch[2]
    arrived = lax.all_to_all(
        mixed.astype(jnp.bfloat16).reshape(spread), "ctx", split_axis=0, concat_axis=0, tiled=True
    )
    convolved = lax.all_to_all(
        convolve(arrived, spectrum, twist, forward, backward), "ctx", split_axis=0, concat_axis=0, tiled=True
    ).reshape(channels, row_count).astype(jnp.float32)
    return (branch[0] * (convolved + skip_gain[:, None] * mixed)).astype(jnp.bfloat16).T


def solution(mesh):
    placed = (
        P("ctx", "tp"),
        P(),
        P(None, None, "tp"),
        P(None, None, "tp"),
        P("ctx", "tp"),
        P("tp"),
    )
    return jax.shard_map(
        body, mesh=mesh, in_specs=placed, out_specs=P("ctx", "tp"), check_vma=False
    )
```

```python
import functools
import math

import jax
import jax.numpy as jnp
import numpy as np
from jax import lax
from jax.experimental import pallas as pl
from jax.experimental.pallas import tpu as pltpu
from jax.sharding import PartitionSpec as P

highest = lax.Precision.HIGHEST


def from_behind(array, axis, by):
    devices = lax.axis_size(axis)
    pairs = [(i, i + by) for i in range(devices) if 0 <= i + by < devices]
    return lax.ppermute(array, axis, pairs)


def twist_tables(part_count, row_count):
    row = lax.optimization_barrier(jnp.arange(row_count, dtype=jnp.int32))
    turn = jnp.arange(part_count + 1, dtype=jnp.int32)[:, None] * row[None, :]
    angles = turn.astype(jnp.float32) * (math.pi / (part_count * row_count))
    return (jnp.cos(angles), jnp.sin(angles))


def inner_tables(row_count):
    row = lax.optimization_barrier(jnp.arange(row_count, dtype=jnp.int32))
    turn = row[:, None] * row[None, :] % row_count
    angles = turn.astype(jnp.float32) * (2.0 * math.pi / row_count)
    cos, sin = jnp.cos(angles), jnp.sin(angles)
    forward = jnp.block([[cos, -sin], [sin, cos]])
    backward = jnp.block([[cos, sin], [-sin, cos]])
    return lax.optimization_barrier((forward, forward.astype(jnp.bfloat16), backward.astype(jnp.bfloat16)))


def turn_of(a, k, part_count):
    step = a * k % (2 * part_count)
    cos = math.cos(math.pi * step / part_count)
    sin = math.sin(math.pi * step / part_count)
    return (0.0 if abs(cos) < 1e-12 else cos, 0.0 if abs(sin) < 1e-12 else sin)


def weighted(terms):
    total = None
    for factor, term in terms:
        if factor == 0.0:
            continue
        scaled = term if factor == 1.0 else -term if factor == -1.0 else factor * term
        total = scaled if total is None else total + scaled
    return total


def filter_spectrum(taps, part_count, twist, forward):
    channels, row_count = taps.shape[1:]
    twist_cos, twist_sin = twist
    turn = np.arange(part_count + 1)[:, None] * np.arange(part_count)[None, :] % (2 * part_count)
    outer_cos = np.cos(turn * (math.pi / part_count)).astype(np.float32)
    outer_sin = np.sin(turn * (math.pi / part_count)).astype(np.float32)
    real = jnp.einsum("ka,acm->kcm", outer_cos, taps, precision=highest)
    imag = -jnp.einsum("ka,acm->kcm", outer_sin, taps, precision=highest)
    cos, sin = twist_cos[:, None, :], twist_sin[:, None, :]
    turned = jnp.concatenate([real * cos + imag * sin, imag * cos - real * sin], axis=2)
    spectrum = jnp.einsum("kcm,mn->kcn", turned, forward, precision=highest)
    share = np.full((part_count + 1, 1, 1), 2.0, np.float32)
    share[0] = share[part_count] = 1.0
    return spectrum * (share / (2 * part_count * row_count))


def convolve_kernel(part_count, x_ref, gain_ref, cos_ref, sin_ref, forward_ref, backward_ref, y_ref, turned_ref, back_ref):
    channels, row_count = x_ref.shape[1:]
    low, high = pl.ds(0, row_count), pl.ds(row_count, row_count)
    parts = [x_ref[a].astype(jnp.float32) for a in range(part_count)]
    for k in range(part_count + 1):
        turns = [turn_of(a, k, part_count) for a in range(part_count)]
        cos, sin = cos_ref[pl.ds(k, 1), :], sin_ref[pl.ds(k, 1), :]
        real = weighted([(t[0], p) for t, p in zip(turns, parts)])
        imag = weighted([(-t[1], p) for t, p in zip(turns, parts)])
        rows = pl.ds(k * channels, channels)
        if imag is None:
            turned_ref[rows, low] = (real * cos).astype(jnp.bfloat16)
            turned_ref[rows, high] = (-real * sin).astype(jnp.bfloat16)
        else:
            turned_ref[rows, low] = (real * cos + imag * sin).astype(jnp.bfloat16)
            turned_ref[rows, high] = (imag * cos - real * sin).astype(jnp.bfloat16)
    spec = jnp.dot(turned_ref[...], forward_ref[...], preferred_element_type=jnp.float32)
    gain = gain_ref[...]
    spec_real, spec_imag = spec[:, :row_count], spec[:, row_count:]
    gain_real, gain_imag = gain[:, :row_count], gain[:, row_count:]
    turned_ref[:, low] = (spec_real * gain_real - spec_imag * gain_imag).astype(jnp.bfloat16)
    turned_ref[:, high] = (spec_real * gain_imag + spec_imag * gain_real).astype(jnp.bfloat16)
    back_ref[...] = jnp.dot(turned_ref[...], backward_ref[...], preferred_element_type=jnp.float32)
    for k in range(part_count + 1):
        cos, sin = cos_ref[pl.ds(k, 1), :], sin_ref[pl.ds(k, 1), :]
        rows = pl.ds(k * channels, channels)
        real, imag = back_ref[rows, low], back_ref[rows, high]
        back_ref[rows, low] = real * cos - imag * sin
        if 0 < k < part_count:
            back_ref[rows, high] = real * sin + imag * cos
    for a in range(part_count):
        terms = []
        for k in range(part_count + 1):
            cos, sin = turn_of(a, k, part_count)
            rows = pl.ds(k * channels, channels)
            terms.append((cos, back_ref[rows, low]))
            if sin != 0.0:
                terms.append((-sin, back_ref[rows, high]))
        y_ref[a] = weighted(terms).astype(jnp.bfloat16)


def convolve(signal, spectrum, twist, forward, backward):
    part_count, channels, row_count = signal.shape
    rows = (part_count + 1) * channels
    return pl.pallas_call(
        functools.partial(convolve_kernel, part_count),
        out_shape=jax.ShapeDtypeStruct(signal.shape, jnp.bfloat16),
        in_specs=[pl.BlockSpec(memory_space=pltpu.VMEM)] * 6,
        out_specs=pl.BlockSpec(memory_space=pltpu.VMEM),
        scratch_shapes=[
            pltpu.VMEM((rows, 2 * row_count), jnp.bfloat16),
            pltpu.VMEM((rows, 2 * row_count), jnp.float32),
        ],
        compiler_params=pltpu.CompilerParams(vmem_limit_bytes=40 << 20),
        name="convolve",
    )(
        signal,
        spectrum.reshape(rows, 2 * row_count),
        *twist,
        forward,
        backward,
    )


def ring_projection(tokens, norm_gain, proj_weight, beside):
    devices, me = lax.axis_size("tp"), lax.axis_index("tp")
    width = tokens.shape[1]
    half = width // 2
    upward = [(i, (i + 1) % devices) for i in range(devices)]
    downward = [(i, (i - 1) % devices) for i in range(devices)]
    halves = [tokens[:, :half], tokens[:, half:]]
    widened = tokens.astype(jnp.float32)
    squares = lax.psum(jnp.sum(widened * widened, axis=1), "tp")
    scaling = lax.rsqrt(squares / (width * devices) + 1e-06)[:, None]
    total = None
    for step in range(devices):
        if step > 0:
            halves = [lax.ppermute(halves[0], "tp", upward), lax.ppermute(halves[1], "tp", downward)]
        owners = [(me - step + devices) % devices, (me + step) % devices]
        firsts = [owners[side] * width + side * half for side in range(2)]
        gain = jnp.concatenate([lax.dynamic_slice_in_dim(norm_gain, first, half, 0) for first in firsts])
        weight = jnp.concatenate(
            [lax.dynamic_slice_in_dim(proj_weight, first, half, 1) for first in firsts], axis=1
        )
        if step == devices - 1:
            halves, total, gain, weight, beside = lax.optimization_barrier(
                (halves, total, gain, weight, beside)
            )
        held = jnp.concatenate(halves, axis=1)
        normed = (held.astype(jnp.float32) * scaling * gain).astype(jnp.bfloat16)
        term = jnp.einsum("td,bdc->bct", normed, weight, preferred_element_type=jnp.float32)
        total = term if total is None else total + term
    return total, beside


def body(tokens, norm_gain, proj_weight, short_taps, long_filter, skip_gain):
    part_count = lax.axis_size("ctx")
    row_count, channels = long_filter.shape
    spread = (part_count, channels // part_count, row_count)
    taps = lax.all_to_all(long_filter.T.reshape(spread), "ctx", split_axis=0, concat_axis=0, tiled=True)
    twist = twist_tables(part_count, row_count)
    inner, forward, backward = inner_tables(row_count)
    spectrum = filter_spectrum(taps, part_count, twist, inner)
    projected, spectrum = ring_projection(tokens, norm_gain, proj_weight, spectrum)
    projected = projected.astype(jnp.bfloat16)
    previous = from_behind(projected[:, :, -2:], "ctx", 1)
    extended = jnp.concatenate([previous, projected], axis=2).astype(jnp.float32)
    branch = (
        short_taps[:, 0, :, None] * extended[:, :, 2:]
        + short_taps[:, 1, :, None] * extended[:, :, 1:-1]
        + short_taps[:, 2, :, None] * extended[:, :, :-2]
    )
    mixed = branch[1] * branch[2]
    arrived = lax.all_to_all(
        mixed.astype(jnp.bfloat16).reshape(spread), "ctx", split_axis=0, concat_axis=0, tiled=True
    )
    convolved = lax.all_to_all(
        convolve(arrived, spectrum, twist, forward, backward), "ctx", split_axis=0, concat_axis=0, tiled=True
    ).reshape(channels, row_count).astype(jnp.float32)
    return (branch[0] * (convolved + skip_gain[:, None] * mixed)).astype(jnp.bfloat16).T


def solution(mesh):
    placed = (
        P("ctx", "tp"),
        P(),
        P(None, None, "tp"),
        P(None, None, "tp"),
        P("ctx", "tp"),
        P("tp"),
    )
    return jax.shard_map(
        body, mesh=mesh, in_specs=placed, out_specs=P("ctx", "tp"), check_vma=False
    )
```

```python
import functools
import math

import jax
import jax.numpy as jnp
import numpy as np
from jax import lax
from jax.experimental import pallas as pl
from jax.experimental.pallas import tpu as pltpu
from jax.sharding import PartitionSpec as P

highest = lax.Precision.HIGHEST


def from_behind(array, axis, by):
    devices = lax.axis_size(axis)
    pairs = [(i, i + by) for i in range(devices) if 0 <= i + by < devices]
    return lax.ppermute(array, axis, pairs)


def twist_tables(part_count, row_count):
    row = lax.optimization_barrier(jnp.arange(row_count, dtype=jnp.int32))
    turn = jnp.arange(part_count + 1, dtype=jnp.int32)[:, None] * row[None, :]
    angles = turn.astype(jnp.float32) * (math.pi / (part_count * row_count))
    return (jnp.cos(angles), jnp.sin(angles))


def inner_tables(row_count):
    row = lax.optimization_barrier(jnp.arange(row_count, dtype=jnp.int32))
    turn = row[:, None] * row[None, :] % row_count
    angles = turn.astype(jnp.float32) * (2.0 * math.pi / row_count)
    cos, sin = jnp.cos(angles), jnp.sin(angles)
    forward = jnp.block([[cos, -sin], [sin, cos]])
    backward = jnp.block([[cos, sin], [-sin, cos]])
    return lax.optimization_barrier((forward, forward.astype(jnp.bfloat16), backward.astype(jnp.bfloat16)))


def turn_of(a, k, part_count):
    step = a * k % (2 * part_count)
    cos = math.cos(math.pi * step / part_count)
    sin = math.sin(math.pi * step / part_count)
    return (0.0 if abs(cos) < 1e-12 else cos, 0.0 if abs(sin) < 1e-12 else sin)


def weighted(terms):
    total = None
    for factor, term in terms:
        if factor == 0.0:
            continue
        scaled = term if factor == 1.0 else -term if factor == -1.0 else factor * term
        total = scaled if total is None else total + scaled
    return total


def filter_spectrum(taps, part_count, twist, forward):
    channels, row_count = taps.shape[1:]
    twist_cos, twist_sin = twist
    turn = np.arange(part_count + 1)[:, None] * np.arange(part_count)[None, :] % (2 * part_count)
    outer_cos = np.cos(turn * (math.pi / part_count)).astype(np.float32)
    outer_sin = np.sin(turn * (math.pi / part_count)).astype(np.float32)
    real = jnp.einsum("ka,acm->kcm", outer_cos, taps, precision=highest)
    imag = -jnp.einsum("ka,acm->kcm", outer_sin, taps, precision=highest)
    cos, sin = twist_cos[:, None, :], twist_sin[:, None, :]
    turned = jnp.concatenate([real * cos + imag * sin, imag * cos - real * sin], axis=2)
    spectrum = jnp.einsum("kcm,mn->kcn", turned, forward, precision=highest)
    share = np.full((part_count + 1, 1, 1), 2.0, np.float32)
    share[0] = share[part_count] = 1.0
    return spectrum * (share / (2 * part_count * row_count))


def to_peers(part_count, me, source, target, send_sem, recv_sem):
    copies = []
    for shift in range(1, part_count):
        peer = lax.rem(me + shift, part_count)
        copies.append(
            pltpu.make_async_remote_copy(
                src_ref=source.at[peer],
                dst_ref=target.at[me],
                send_sem=send_sem.at[peer],
                recv_sem=recv_sem.at[me],
                device_id={"ctx": peer},
                device_id_type=pl.DeviceIdType.MESH,
            )
        )
    return copies


def wait_for_peers(part_count, me, source, target, send_sem, recv_sem):
    for shift in range(1, part_count):
        peer = lax.rem(me + shift, part_count)
        pltpu.make_async_remote_copy(
            src_ref=source.at[peer],
            dst_ref=target.at[peer],
            send_sem=send_sem.at[peer],
            recv_sem=recv_sem.at[peer],
            device_id={"ctx": peer},
            device_id_type=pl.DeviceIdType.MESH,
        ).wait_recv()


def convolve_kernel(
    part_count, mixed_ref, gate_ref, skip_ref, cos_ref, sin_ref, gain_any, forward_any, backward_any, out_ref,
    sent_ref, x_ref, y_ref, z_ref, gain_ref, forward_ref, backward_ref, turned_ref, back_ref,
    local_sem, send_x, recv_x, send_y, recv_y,
):
    me = lax.axis_index("ctx")
    loads = [
        pltpu.make_async_copy(source, target, local_sem.at[i])
        for i, (source, target) in enumerate(
            [(forward_any, forward_ref), (gain_any, gain_ref), (backward_any, backward_ref)]
        )
    ]
    for load in loads:
        load.start()
    barrier = pltpu.get_barrier_semaphore()
    for shift in range(1, part_count):
        pl.semaphore_signal(
            barrier, inc=1, device_id={"ctx": lax.rem(me + shift, part_count)},
            device_id_type=pl.DeviceIdType.MESH,
        )
    sent_ref[...] = mixed_ref[...].astype(jnp.bfloat16)
    pl.semaphore_wait(barrier, part_count - 1)
    out_x = to_peers(part_count, me, sent_ref, x_ref, send_x, recv_x)
    for copy in out_x:
        copy.start()
    x_ref[me] = sent_ref[me]
    wait_for_peers(part_count, me, sent_ref, x_ref, send_x, recv_x)
    channels, row_count = x_ref.shape[1:]
    low, high = pl.ds(0, row_count), pl.ds(row_count, row_count)
    parts = [x_ref[a].astype(jnp.float32) for a in range(part_count)]
    for k in range(part_count + 1):
        turns = [turn_of(a, k, part_count) for a in range(part_count)]
        cos, sin = cos_ref[pl.ds(k, 1), :], sin_ref[pl.ds(k, 1), :]
        real = weighted([(t[0], p) for t, p in zip(turns, parts)])
        imag = weighted([(-t[1], p) for t, p in zip(turns, parts)])
        rows = pl.ds(k * channels, channels)
        if imag is None:
            turned_ref[rows, low] = (real * cos).astype(jnp.bfloat16)
            turned_ref[rows, high] = (-real * sin).astype(jnp.bfloat16)
        else:
            turned_ref[rows, low] = (real * cos + imag * sin).astype(jnp.bfloat16)
            turned_ref[rows, high] = (imag * cos - real * sin).astype(jnp.bfloat16)
    loads[0].wait()
    loads[1].wait()
    spec = jnp.dot(turned_ref[...], forward_ref[...], preferred_element_type=jnp.float32)
    gain = gain_ref[...]
    spec_real, spec_imag = spec[:, :row_count], spec[:, row_count:]
    gain_real, gain_imag = gain[:, :row_count], gain[:, row_count:]
    turned_ref[:, low] = (spec_real * gain_real - spec_imag * gain_imag).astype(jnp.bfloat16)
    turned_ref[:, high] = (spec_real * gain_imag + spec_imag * gain_real).astype(jnp.bfloat16)
    loads[2].wait()
    back_ref[...] = jnp.dot(turned_ref[...], backward_ref[...], preferred_element_type=jnp.float32)
    for k in range(part_count + 1):
        cos, sin = cos_ref[pl.ds(k, 1), :], sin_ref[pl.ds(k, 1), :]
        rows = pl.ds(k * channels, channels)
        real, imag = back_ref[rows, low], back_ref[rows, high]
        back_ref[rows, low] = real * cos - imag * sin
        if 0 < k < part_count:
            back_ref[rows, high] = real * sin + imag * cos
    for a in range(part_count):
        terms = []
        for k in range(part_count + 1):
            cos, sin = turn_of(a, k, part_count)
            rows = pl.ds(k * channels, channels)
            terms.append((cos, back_ref[rows, low]))
            if sin != 0.0:
                terms.append((-sin, back_ref[rows, high]))
        y_ref[a] = weighted(terms).astype(jnp.bfloat16)
    out_y = to_peers(part_count, me, y_ref, z_ref, send_y, recv_y)
    for copy in out_y:
        copy.start()
    z_ref[me] = y_ref[me]
    wait_for_peers(part_count, me, y_ref, z_ref, send_y, recv_y)
    for p in range(part_count):
        rows = pl.ds(p * channels, channels)
        gated = gate_ref[p] * (z_ref[p].astype(jnp.float32) + skip_ref[rows, :] * mixed_ref[p])
        out_ref[p] = gated.astype(jnp.bfloat16)
    for copy in out_x + out_y:
        copy.wait_send()


def convolve(mixed, gate, skip_gain, spectrum, twist, forward, backward):
    part_count, channels, row_count = mixed.shape
    rows = (part_count + 1) * channels
    held = pl.BlockSpec(memory_space=pltpu.VMEM)
    block = (part_count, channels, row_count)
    square = (2 * row_count, 2 * row_count)
    return pl.pallas_call(
        functools.partial(convolve_kernel, part_count),
        out_shape=jax.ShapeDtypeStruct(block, jnp.bfloat16),
        in_specs=[held] * 5 + [pl.BlockSpec(memory_space=pl.ANY)] * 3,
        out_specs=held,
        scratch_shapes=[pltpu.VMEM(block, jnp.bfloat16)] * 4
        + [
            pltpu.VMEM((rows, 2 * row_count), jnp.float32),
            pltpu.VMEM(square, jnp.bfloat16),
            pltpu.VMEM(square, jnp.bfloat16),
            pltpu.VMEM((rows, 2 * row_count), jnp.bfloat16),
            pltpu.VMEM((rows, 2 * row_count), jnp.float32),
            pltpu.SemaphoreType.DMA((3,)),
        ]
        + [pltpu.SemaphoreType.DMA((part_count,))] * 4,
        compiler_params=pltpu.CompilerParams(
            vmem_limit_bytes=44 << 20, collective_id=0, has_side_effects=True
        ),
        name="convolve",
    )(mixed, gate, skip_gain[:, None], *twist, spectrum.reshape(rows, 2 * row_count), forward, backward)


def body(tokens, norm_gain, proj_weight, short_taps, long_filter, skip_gain):
    part_count = lax.axis_size("ctx")
    row_count, channels = long_filter.shape
    spread = (part_count, channels // part_count, row_count)
    gathered = lax.all_gather(tokens, "tp", axis=1, tiled=True)
    taps = lax.all_to_all(long_filter.T.reshape(spread), "ctx", split_axis=0, concat_axis=0, tiled=True)
    twist = twist_tables(part_count, row_count)
    inner, forward, backward = inner_tables(row_count)
    spectrum = filter_spectrum(taps, part_count, twist, inner)
    gathered, spectrum = lax.optimization_barrier((gathered, spectrum))
    widened = gathered.astype(jnp.float32)
    scaling = lax.rsqrt(jnp.mean(widened * widened, axis=1, keepdims=True) + 1e-06)
    normed = (widened * scaling * norm_gain).astype(jnp.bfloat16)
    projected = jnp.einsum(
        "td,bdc->bct", normed, proj_weight, preferred_element_type=jnp.float32
    ).astype(jnp.bfloat16)
    previous = from_behind(projected[:, :, -2:], "ctx", 1)
    extended = jnp.concatenate([previous, projected], axis=2).astype(jnp.float32)
    branch = (
        short_taps[:, 0, :, None] * extended[:, :, 2:]
        + short_taps[:, 1, :, None] * extended[:, :, 1:-1]
        + short_taps[:, 2, :, None] * extended[:, :, :-2]
    )
    mixed = branch[1] * branch[2]
    result = convolve(
        mixed.reshape(spread), branch[0].reshape(spread), skip_gain, spectrum, twist, forward, backward
    )
    return result.reshape(channels, row_count).T


def solution(mesh):
    placed = (
        P("ctx", "tp"),
        P(),
        P(None, None, "tp"),
        P(None, None, "tp"),
        P("ctx", "tp"),
        P("tp"),
    )
    return jax.shard_map(
        body, mesh=mesh, in_specs=placed, out_specs=P("ctx", "tp"), check_vma=False
    )
```

```python
import functools
import math

import jax
import jax.numpy as jnp
import numpy as np
from jax import lax
from jax.experimental import pallas as pl
from jax.experimental.pallas import tpu as pltpu
from jax.sharding import PartitionSpec as P

highest = lax.Precision.HIGHEST


def twist_tables(part_count, row_count):
    row = lax.optimization_barrier(jnp.arange(row_count, dtype=jnp.int32))
    turn = jnp.arange(part_count + 1, dtype=jnp.int32)[:, None] * row[None, :]
    angles = turn.astype(jnp.float32) * (math.pi / (part_count * row_count))
    return (jnp.cos(angles), jnp.sin(angles))


def inner_tables(row_count):
    row = lax.optimization_barrier(jnp.arange(row_count, dtype=jnp.int32))
    turn = row[:, None] * row[None, :] % row_count
    angles = turn.astype(jnp.float32) * (2.0 * math.pi / row_count)
    cos, sin = jnp.cos(angles), jnp.sin(angles)
    forward = jnp.block([[cos, -sin], [sin, cos]])
    backward = jnp.block([[cos, sin], [-sin, cos]])
    return lax.optimization_barrier((forward, forward.astype(jnp.bfloat16), backward.astype(jnp.bfloat16)))


def turn_of(a, k, part_count):
    step = a * k % (2 * part_count)
    cos = math.cos(math.pi * step / part_count)
    sin = math.sin(math.pi * step / part_count)
    return (0.0 if abs(cos) < 1e-12 else cos, 0.0 if abs(sin) < 1e-12 else sin)


def weighted(terms):
    total = None
    for factor, term in terms:
        if factor == 0.0:
            continue
        scaled = term if factor == 1.0 else -term if factor == -1.0 else factor * term
        total = scaled if total is None else total + scaled
    return total


def filter_spectrum(taps, part_count, twist, forward):
    channels, row_count = taps.shape[1:]
    twist_cos, twist_sin = twist
    turn = np.arange(part_count + 1)[:, None] * np.arange(part_count)[None, :] % (2 * part_count)
    outer_cos = np.cos(turn * (math.pi / part_count)).astype(np.float32)
    outer_sin = np.sin(turn * (math.pi / part_count)).astype(np.float32)
    real = jnp.einsum("ka,acm->kcm", outer_cos, taps, precision=highest)
    imag = -jnp.einsum("ka,acm->kcm", outer_sin, taps, precision=highest)
    cos, sin = twist_cos[:, None, :], twist_sin[:, None, :]
    turned = jnp.concatenate([real * cos + imag * sin, imag * cos - real * sin], axis=2)
    spectrum = jnp.einsum("kcm,mn->kcn", turned, forward, precision=highest)
    share = np.full((part_count + 1, 1, 1), 2.0, np.float32)
    share[0] = share[part_count] = 1.0
    return spectrum * (share / (2 * part_count * row_count))


def to_peers(part_count, me, source, target, send_sem, recv_sem):
    copies = []
    for shift in range(1, part_count):
        peer = lax.rem(me + shift, part_count)
        copies.append(
            pltpu.make_async_remote_copy(
                src_ref=source.at[peer],
                dst_ref=target.at[me],
                send_sem=send_sem.at[peer],
                recv_sem=recv_sem.at[me],
                device_id={"ctx": peer},
                device_id_type=pl.DeviceIdType.MESH,
            )
        )
    return copies


def wait_for_peers(part_count, me, source, target, send_sem, recv_sem):
    for shift in range(1, part_count):
        peer = lax.rem(me + shift, part_count)
        pltpu.make_async_remote_copy(
            src_ref=source.at[peer],
            dst_ref=target.at[peer],
            send_sem=send_sem.at[peer],
            recv_sem=recv_sem.at[peer],
            device_id={"ctx": peer},
            device_id_type=pl.DeviceIdType.MESH,
        ).wait_recv()


def convolve_kernel(
    part_count, proj_ref, taps_ref, skip_ref, cos_ref, sin_ref, gain_any, forward_any, backward_any, out_ref,
    halo_ref, wide_ref, mixed_ref, gate_ref, sent_ref, x_ref, y_ref, z_ref, gain_ref, forward_ref,
    backward_ref, turned_ref, back_ref, local_sem, halo_sem, send_x, recv_x, send_y, recv_y,
):
    channels, row_count = x_ref.shape[1:]
    width = proj_ref.shape[2]
    chunk = min(width, max(128, channels))
    blocks = chunk // channels
    me = lax.axis_index("ctx")
    loads = [
        pltpu.make_async_copy(source, target, local_sem.at[i])
        for i, (source, target) in enumerate(
            [(forward_any, forward_ref), (gain_any, gain_ref), (backward_any, backward_ref)]
        )
    ]
    for load in loads:
        load.start()
    barrier = pltpu.get_barrier_semaphore()
    for shift in range(1, part_count):
        pl.semaphore_signal(
            barrier, inc=1, device_id={"ctx": lax.rem(me + shift, part_count)},
            device_id_type=pl.DeviceIdType.MESH,
        )
    halo = pltpu.make_async_remote_copy(
        src_ref=proj_ref.at[:, pl.ds(row_count - 16, 16), :],
        dst_ref=halo_ref,
        send_sem=halo_sem.at[0],
        recv_sem=halo_sem.at[1],
        device_id={"ctx": lax.rem(me + 1, part_count)},
        device_id_type=pl.DeviceIdType.MESH,
    )
    pl.semaphore_wait(barrier, part_count - 1)
    halo.start()
    for i in range(3):
        wide_ref[i, pl.ds(8, row_count), :] = proj_ref[i].astype(jnp.float32)
    halo.wait()
    for i in range(3):
        before = halo_ref[i].astype(jnp.float32)[8:]
        wide_ref[i, pl.ds(0, 8), :] = jnp.where(me > 0, before, jnp.zeros_like(before))

    def branch(i, columns):
        return (
            taps_ref[i, pl.ds(0, 1), columns] * wide_ref[i, pl.ds(8, row_count), columns]
            + taps_ref[i, pl.ds(1, 1), columns] * wide_ref[i, pl.ds(7, row_count), columns]
            + taps_ref[i, pl.ds(2, 1), columns] * wide_ref[i, pl.ds(6, row_count), columns]
        )

    for j in range(width // chunk):
        columns = pl.ds(j * chunk, chunk)
        mixed = branch(1, columns) * branch(2, columns)
        mixed_ref[:, columns] = mixed
        sent_ref[pl.ds(j * blocks, blocks)] = (
            jnp.transpose(mixed).astype(jnp.bfloat16).reshape(blocks, channels, row_count)
        )
    out_x = to_peers(part_count, me, sent_ref, x_ref, send_x, recv_x)
    for copy in out_x:
        copy.start()
    x_ref[me] = sent_ref[me]
    for j in range(width // chunk):
        columns = pl.ds(j * chunk, chunk)
        gate_ref[:, columns] = branch(0, columns)
    wait_for_peers(part_count, me, sent_ref, x_ref, send_x, recv_x)
    low, high = pl.ds(0, row_count), pl.ds(row_count, row_count)
    parts = [x_ref[a].astype(jnp.float32) for a in range(part_count)]
    for k in range(part_count + 1):
        turns = [turn_of(a, k, part_count) for a in range(part_count)]
        cos, sin = cos_ref[pl.ds(k, 1), :], sin_ref[pl.ds(k, 1), :]
        real = weighted([(t[0], p) for t, p in zip(turns, parts)])
        imag = weighted([(-t[1], p) for t, p in zip(turns, parts)])
        rows = pl.ds(k * channels, channels)
        if imag is None:
            turned_ref[rows, low] = (real * cos).astype(jnp.bfloat16)
            turned_ref[rows, high] = (-real * sin).astype(jnp.bfloat16)
        else:
            turned_ref[rows, low] = (real * cos + imag * sin).astype(jnp.bfloat16)
            turned_ref[rows, high] = (imag * cos - real * sin).astype(jnp.bfloat16)
    loads[0].wait()
    loads[1].wait()
    spec = jnp.dot(turned_ref[...], forward_ref[...], preferred_element_type=jnp.float32)
    gain = gain_ref[...]
    spec_real, spec_imag = spec[:, :row_count], spec[:, row_count:]
    gain_real, gain_imag = gain[:, :row_count], gain[:, row_count:]
    turned_ref[:, low] = (spec_real * gain_real - spec_imag * gain_imag).astype(jnp.bfloat16)
    turned_ref[:, high] = (spec_real * gain_imag + spec_imag * gain_real).astype(jnp.bfloat16)
    loads[2].wait()
    back_ref[...] = jnp.dot(turned_ref[...], backward_ref[...], preferred_element_type=jnp.float32)
    for k in range(part_count + 1):
        cos, sin = cos_ref[pl.ds(k, 1), :], sin_ref[pl.ds(k, 1), :]
        rows = pl.ds(k * channels, channels)
        real, imag = back_ref[rows, low], back_ref[rows, high]
        back_ref[rows, low] = real * cos - imag * sin
        if 0 < k < part_count:
            back_ref[rows, high] = real * sin + imag * cos
    for a in range(part_count):
        terms = []
        for k in range(part_count + 1):
            cos, sin = turn_of(a, k, part_count)
            rows = pl.ds(k * channels, channels)
            terms.append((cos, back_ref[rows, low]))
            if sin != 0.0:
                terms.append((-sin, back_ref[rows, high]))
        y_ref[a] = weighted(terms).astype(jnp.bfloat16)
    out_y = to_peers(part_count, me, y_ref, z_ref, send_y, recv_y)
    for copy in out_y:
        copy.start()
    z_ref[me] = y_ref[me]
    wait_for_peers(part_count, me, y_ref, z_ref, send_y, recv_y)
    for j in range(width // chunk):
        columns = pl.ds(j * chunk, chunk)
        arrived = z_ref[pl.ds(j * blocks, blocks)].astype(jnp.float32).reshape(chunk, row_count)
        direct = skip_ref[:, columns] * mixed_ref[:, columns]
        out_ref[:, columns] = (gate_ref[:, columns] * (jnp.transpose(arrived) + direct)).astype(jnp.bfloat16)
    for copy in out_x + out_y:
        copy.wait_send()


def convolve(projected, short_taps, skip_gain, spectrum, twist, forward, backward):
    part_count, channels = spectrum.shape[0] - 1, spectrum.shape[1]
    row_count, width = projected.shape[1:]
    rows = (part_count + 1) * channels
    held = pl.BlockSpec(memory_space=pltpu.VMEM)
    block = (part_count, channels, row_count)
    square = (2 * row_count, 2 * row_count)
    return pl.pallas_call(
        functools.partial(convolve_kernel, part_count),
        out_shape=jax.ShapeDtypeStruct((row_count, width), jnp.bfloat16),
        in_specs=[held] * 5 + [pl.BlockSpec(memory_space=pl.ANY)] * 3,
        out_specs=held,
        scratch_shapes=[
            pltpu.VMEM((3, 16, width), jnp.bfloat16),
            pltpu.VMEM((3, row_count + 8, width), jnp.float32),
            pltpu.VMEM((row_count, width), jnp.float32),
            pltpu.VMEM((row_count, width), jnp.float32),
        ]
        + [pltpu.VMEM(block, jnp.bfloat16)] * 4
        + [
            pltpu.VMEM((rows, 2 * row_count), jnp.float32),
            pltpu.VMEM(square, jnp.bfloat16),
            pltpu.VMEM(square, jnp.bfloat16),
            pltpu.VMEM((rows, 2 * row_count), jnp.bfloat16),
            pltpu.VMEM((rows, 2 * row_count), jnp.float32),
            pltpu.SemaphoreType.DMA((3,)),
            pltpu.SemaphoreType.DMA((2,)),
        ]
        + [pltpu.SemaphoreType.DMA((part_count,))] * 4,
        compiler_params=pltpu.CompilerParams(
            vmem_limit_bytes=56 << 20, collective_id=0, has_side_effects=True
        ),
        name="convolve",
    )(projected, short_taps, skip_gain[None, :], *twist, spectrum.reshape(rows, 2 * row_count), forward, backward)


def body(tokens, norm_gain, proj_weight, short_taps, long_filter, skip_gain):
    part_count = lax.axis_size("ctx")
    row_count, channels = long_filter.shape
    spread = (part_count, channels // part_count, row_count)
    gathered = lax.all_gather(tokens, "tp", axis=1, tiled=True)
    taps = lax.all_to_all(long_filter.T.reshape(spread), "ctx", split_axis=0, concat_axis=0, tiled=True)
    twist = twist_tables(part_count, row_count)
    inner, forward, backward = inner_tables(row_count)
    spectrum = filter_spectrum(taps, part_count, twist, inner)
    gathered, spectrum = lax.optimization_barrier((gathered, spectrum))
    widened = gathered.astype(jnp.float32)
    scaling = lax.rsqrt(jnp.mean(widened * widened, axis=1, keepdims=True) + 1e-06)
    normed = (widened * scaling * norm_gain).astype(jnp.bfloat16)
    projected = jnp.einsum(
        "td,bdc->btc", normed, proj_weight, preferred_element_type=jnp.float32
    ).astype(jnp.bfloat16)
    return convolve(projected, short_taps, skip_gain, spectrum, twist, forward, backward)


def solution(mesh):
    placed = (
        P("ctx", "tp"),
        P(),
        P(None, None, "tp"),
        P(None, None, "tp"),
        P("ctx", "tp"),
        P("tp"),
    )
    return jax.shard_map(
        body, mesh=mesh, in_specs=placed, out_specs=P("ctx", "tp"), check_vma=False
    )
```

```python
import functools
import math

import jax
import jax.numpy as jnp
import numpy as np
from jax import lax
from jax.experimental import pallas as pl
from jax.experimental.pallas import tpu as pltpu
from jax.sharding import PartitionSpec as P

highest = lax.Precision.HIGHEST


def twist_tables(part_count, row_count):
    row = lax.optimization_barrier(jnp.arange(row_count, dtype=jnp.int32))
    turn = jnp.arange(part_count + 1, dtype=jnp.int32)[:, None] * row[None, :]
    angles = turn.astype(jnp.float32) * (math.pi / (part_count * row_count))
    return (jnp.cos(angles), jnp.sin(angles))


def inner_tables(row_count):
    row = lax.optimization_barrier(jnp.arange(row_count, dtype=jnp.int32))
    turn = row[:, None] * row[None, :] % row_count
    angles = turn.astype(jnp.float32) * (2.0 * math.pi / row_count)
    cos, sin = jnp.cos(angles), jnp.sin(angles)
    forward = jnp.block([[cos, -sin], [sin, cos]])
    backward = jnp.block([[cos, sin], [-sin, cos]])
    return lax.optimization_barrier((forward, forward.astype(jnp.bfloat16), backward.astype(jnp.bfloat16)))


def turn_of(a, k, part_count):
    step = a * k % (2 * part_count)
    cos = math.cos(math.pi * step / part_count)
    sin = math.sin(math.pi * step / part_count)
    return (0.0 if abs(cos) < 1e-12 else cos, 0.0 if abs(sin) < 1e-12 else sin)


def weighted(terms):
    total = None
    for factor, term in terms:
        if factor == 0.0:
            continue
        scaled = term if factor == 1.0 else -term if factor == -1.0 else factor * term
        total = scaled if total is None else total + scaled
    return total


def filter_spectrum(taps, part_count, twist, forward):
    channels, row_count = taps.shape[1:]
    twist_cos, twist_sin = twist
    turn = np.arange(part_count + 1)[:, None] * np.arange(part_count)[None, :] % (2 * part_count)
    outer_cos = np.cos(turn * (math.pi / part_count)).astype(np.float32)
    outer_sin = np.sin(turn * (math.pi / part_count)).astype(np.float32)
    real = jnp.einsum("ka,acm->kcm", outer_cos, taps, precision=highest)
    imag = -jnp.einsum("ka,acm->kcm", outer_sin, taps, precision=highest)
    cos, sin = twist_cos[:, None, :], twist_sin[:, None, :]
    turned = jnp.concatenate([real * cos + imag * sin, imag * cos - real * sin], axis=2)
    spectrum = jnp.einsum("kcm,mn->kcn", turned, forward, precision=highest)
    share = np.full((part_count + 1, 1, 1), 2.0, np.float32)
    share[0] = share[part_count] = 1.0
    return spectrum * (share / (2 * part_count * row_count))


def to_peers(part_count, me, source, target, send_sem, recv_sem):
    copies = []
    for shift in range(1, part_count):
        peer = lax.rem(me + shift, part_count)
        copies.append(
            pltpu.make_async_remote_copy(
                src_ref=source.at[peer],
                dst_ref=target.at[me],
                send_sem=send_sem.at[peer],
                recv_sem=recv_sem.at[me],
                device_id={"ctx": peer},
                device_id_type=pl.DeviceIdType.MESH,
            )
        )
    return copies


def wait_for_peers(part_count, me, source, target, send_sem, recv_sem):
    for shift in range(1, part_count):
        peer = lax.rem(me + shift, part_count)
        pltpu.make_async_remote_copy(
            src_ref=source.at[peer],
            dst_ref=target.at[peer],
            send_sem=send_sem.at[peer],
            recv_sem=recv_sem.at[peer],
            device_id={"ctx": peer},
            device_id_type=pl.DeviceIdType.MESH,
        ).wait_recv()


def convolve_kernel(
    part_count, first_ref, second_ref, taps_ref, skip_ref, cos_ref, sin_ref, gain_any, forward_any, backward_any, out_ref,
    halo_ref, wide_ref, mixed_ref, gate_ref, sent_ref, x_ref, y_ref, z_ref, gain_ref, forward_ref,
    backward_ref, turned_ref, back_ref, local_sem, halo_sem, send_x, recv_x, send_y, recv_y,
):
    channels, row_count = x_ref.shape[1:]
    half, width = first_ref.shape[1:]
    chunk = min(width, max(128, channels))
    blocks = chunk // channels
    me = lax.axis_index("ctx")
    loads = [
        pltpu.make_async_copy(source, target, local_sem.at[i])
        for i, (source, target) in enumerate(
            [(forward_any, forward_ref), (gain_any, gain_ref), (backward_any, backward_ref)]
        )
    ]
    for load in loads:
        load.start()
    barrier = pltpu.get_barrier_semaphore()
    for shift in range(1, part_count):
        pl.semaphore_signal(
            barrier, inc=1, device_id={"ctx": lax.rem(me + shift, part_count)},
            device_id_type=pl.DeviceIdType.MESH,
        )
    halo = pltpu.make_async_remote_copy(
        src_ref=second_ref.at[:, pl.ds(half - 16, 16), :],
        dst_ref=halo_ref,
        send_sem=halo_sem.at[0],
        recv_sem=halo_sem.at[1],
        device_id={"ctx": lax.rem(me + 1, part_count)},
        device_id_type=pl.DeviceIdType.MESH,
    )
    pl.semaphore_wait(barrier, part_count - 1)
    halo.start()
    for i in range(3):
        wide_ref[i, pl.ds(8, half), :] = first_ref[i].astype(jnp.float32)
        wide_ref[i, pl.ds(8 + half, half), :] = second_ref[i].astype(jnp.float32)
    halo.wait()
    for i in range(3):
        before = halo_ref[i].astype(jnp.float32)[8:]
        wide_ref[i, pl.ds(0, 8), :] = jnp.where(me > 0, before, jnp.zeros_like(before))

    def branch(i, columns):
        return (
            taps_ref[i, pl.ds(0, 1), columns] * wide_ref[i, pl.ds(8, row_count), columns]
            + taps_ref[i, pl.ds(1, 1), columns] * wide_ref[i, pl.ds(7, row_count), columns]
            + taps_ref[i, pl.ds(2, 1), columns] * wide_ref[i, pl.ds(6, row_count), columns]
        )

    for j in range(width // chunk):
        columns = pl.ds(j * chunk, chunk)
        mixed = branch(1, columns) * branch(2, columns)
        mixed_ref[:, columns] = mixed
        sent_ref[pl.ds(j * blocks, blocks)] = (
            jnp.transpose(mixed).astype(jnp.bfloat16).reshape(blocks, channels, row_count)
        )
    out_x = to_peers(part_count, me, sent_ref, x_ref, send_x, recv_x)
    for copy in out_x:
        copy.start()
    x_ref[me] = sent_ref[me]
    for j in range(width // chunk):
        columns = pl.ds(j * chunk, chunk)
        gate_ref[:, columns] = branch(0, columns)
    wait_for_peers(part_count, me, sent_ref, x_ref, send_x, recv_x)
    low, high = pl.ds(0, row_count), pl.ds(row_count, row_count)
    parts = [x_ref[a].astype(jnp.float32) for a in range(part_count)]
    for k in range(part_count + 1):
        turns = [turn_of(a, k, part_count) for a in range(part_count)]
        cos, sin = cos_ref[pl.ds(k, 1), :], sin_ref[pl.ds(k, 1), :]
        real = weighted([(t[0], p) for t, p in zip(turns, parts)])
        imag = weighted([(-t[1], p) for t, p in zip(turns, parts)])
        rows = pl.ds(k * channels, channels)
        if imag is None:
            turned_ref[rows, low] = (real * cos).astype(jnp.bfloat16)
            turned_ref[rows, high] = (-real * sin).astype(jnp.bfloat16)
        else:
            turned_ref[rows, low] = (real * cos + imag * sin).astype(jnp.bfloat16)
            turned_ref[rows, high] = (imag * cos - real * sin).astype(jnp.bfloat16)
    loads[0].wait()
    loads[1].wait()
    spec = jnp.dot(turned_ref[...], forward_ref[...], preferred_element_type=jnp.float32)
    gain = gain_ref[...]
    spec_real, spec_imag = spec[:, :row_count], spec[:, row_count:]
    gain_real, gain_imag = gain[:, :row_count], gain[:, row_count:]
    turned_ref[:, low] = (spec_real * gain_real - spec_imag * gain_imag).astype(jnp.bfloat16)
    turned_ref[:, high] = (spec_real * gain_imag + spec_imag * gain_real).astype(jnp.bfloat16)
    loads[2].wait()
    back_ref[...] = jnp.dot(turned_ref[...], backward_ref[...], preferred_element_type=jnp.float32)
    for k in range(part_count + 1):
        cos, sin = cos_ref[pl.ds(k, 1), :], sin_ref[pl.ds(k, 1), :]
        rows = pl.ds(k * channels, channels)
        real, imag = back_ref[rows, low], back_ref[rows, high]
        back_ref[rows, low] = real * cos - imag * sin
        if 0 < k < part_count:
            back_ref[rows, high] = real * sin + imag * cos
    for a in range(part_count):
        terms = []
        for k in range(part_count + 1):
            cos, sin = turn_of(a, k, part_count)
            rows = pl.ds(k * channels, channels)
            terms.append((cos, back_ref[rows, low]))
            if sin != 0.0:
                terms.append((-sin, back_ref[rows, high]))
        y_ref[a] = weighted(terms).astype(jnp.bfloat16)
    out_y = to_peers(part_count, me, y_ref, z_ref, send_y, recv_y)
    for copy in out_y:
        copy.start()
    z_ref[me] = y_ref[me]
    wait_for_peers(part_count, me, y_ref, z_ref, send_y, recv_y)
    for j in range(width // chunk):
        columns = pl.ds(j * chunk, chunk)
        arrived = z_ref[pl.ds(j * blocks, blocks)].astype(jnp.float32).reshape(chunk, row_count)
        direct = skip_ref[:, columns] * mixed_ref[:, columns]
        out_ref[:, columns] = (gate_ref[:, columns] * (jnp.transpose(arrived) + direct)).astype(jnp.bfloat16)
    for copy in out_x + out_y:
        copy.wait_send()


def convolve(first, second, short_taps, skip_gain, spectrum, twist, forward, backward):
    part_count, channels = spectrum.shape[0] - 1, spectrum.shape[1]
    row_count, width = 2 * first.shape[1], first.shape[2]
    rows = (part_count + 1) * channels
    held = pl.BlockSpec(memory_space=pltpu.VMEM)
    block = (part_count, channels, row_count)
    square = (2 * row_count, 2 * row_count)
    return pl.pallas_call(
        functools.partial(convolve_kernel, part_count),
        out_shape=jax.ShapeDtypeStruct((row_count, width), jnp.bfloat16),
        in_specs=[held] * 6 + [pl.BlockSpec(memory_space=pl.ANY)] * 3,
        out_specs=held,
        scratch_shapes=[
            pltpu.VMEM((3, 16, width), jnp.bfloat16),
            pltpu.VMEM((3, row_count + 8, width), jnp.float32),
            pltpu.VMEM((row_count, width), jnp.float32),
            pltpu.VMEM((row_count, width), jnp.float32),
        ]
        + [pltpu.VMEM(block, jnp.bfloat16)] * 4
        + [
            pltpu.VMEM((rows, 2 * row_count), jnp.float32),
            pltpu.VMEM(square, jnp.bfloat16),
            pltpu.VMEM(square, jnp.bfloat16),
            pltpu.VMEM((rows, 2 * row_count), jnp.bfloat16),
            pltpu.VMEM((rows, 2 * row_count), jnp.float32),
            pltpu.SemaphoreType.DMA((3,)),
            pltpu.SemaphoreType.DMA((2,)),
        ]
        + [pltpu.SemaphoreType.DMA((part_count,))] * 4,
        compiler_params=pltpu.CompilerParams(
            vmem_limit_bytes=56 << 20, collective_id=0, has_side_effects=True
        ),
        name="convolve",
    )(first, second, short_taps, skip_gain[None, :], *twist, spectrum.reshape(rows, 2 * row_count), forward, backward)


def project(gathered, norm_gain, proj_weight):
    widened = gathered.astype(jnp.float32)
    scaling = lax.rsqrt(jnp.mean(widened * widened, axis=1, keepdims=True) + 1e-06)
    normed = (widened * scaling * norm_gain).astype(jnp.bfloat16)
    return jnp.einsum(
        "td,bdc->btc", normed, proj_weight, preferred_element_type=jnp.float32
    ).astype(jnp.bfloat16)


def body(tokens, norm_gain, proj_weight, short_taps, long_filter, skip_gain):
    part_count = lax.axis_size("ctx")
    row_count, channels = long_filter.shape
    spread = (part_count, channels // part_count, row_count)
    half = row_count // 2
    early = lax.all_gather(tokens[:half], "tp", axis=1, tiled=True)
    late = lax.all_gather(tokens[half:], "tp", axis=1, tiled=True)
    taps = lax.all_to_all(long_filter.T.reshape(spread), "ctx", split_axis=0, concat_axis=0, tiled=True)
    twist = twist_tables(part_count, row_count)
    inner, forward, backward = inner_tables(row_count)
    spectrum = filter_spectrum(taps, part_count, twist, inner)
    early, spectrum = lax.optimization_barrier((early, spectrum))
    first = project(early, norm_gain, proj_weight)
    late, first = lax.optimization_barrier((late, first))
    second = project(late, norm_gain, proj_weight)
    return convolve(first, second, short_taps, skip_gain, spectrum, twist, forward, backward)


def solution(mesh):
    placed = (
        P("ctx", "tp"),
        P(),
        P(None, None, "tp"),
        P(None, None, "tp"),
        P("ctx", "tp"),
        P("tp"),
    )
    return jax.shard_map(
        body, mesh=mesh, in_specs=placed, out_specs=P("ctx", "tp"), check_vma=False
    )
```
